256 devices in a mesh: row: 16 (over y_hi, x, core), col: 16 (over y_lo, z).
Axes of the slice: x: 4, y: 4 (y_hi: 2, y_lo: 2; y = y_hi * 2 + y_lo), z: 8, core: 2. Of those that a mesh axis runs over, the one named last changes fastest.
Arguments:
- x_blocks: bfloat16 [16, 16, 16, 128, 128], P('row', 'col'), may hold values from -0.8984375 to 0.8984375
- x_live: int32 [16, 16, 16], P('row', 'col'), may hold values 0 or 1
- pair_slots: int32 [16, 16, 4, 3, 192], P('row', 'col'), may hold values from 0 to 15
- pair_count: int32 [16, 16, 4], P('row', 'col'), may hold values from 15 to 192, as said below
Outputs:
- gram_blocks: float32 [16, 16, 16, 128, 128], P('row', 'col')
The draws below stay inside these ranges and needn't reach their ends.
Inputs may be any that keep to these rules, and one draw needn't show every extreme that they name: `pair_count`: live pairs of a tile at a section; some tile has exactly 192 at its first section.
All inputs are finite; a program needn't handle non-finite values. No bound on the sum of `x_live` on one device may be relied on, other than what follows from the above.
Results may differ from the reference program's by a relative error of at most 0.0003.
Values may be sent and summed in bfloat16 or wider, within the bound.
A program may use at most 64 MiB of HBM per device.

```python
import jax
import jax.numpy as jnp
from jax import lax

BLK = 128
SLOTS = 16
PAIRS = 192
SECTIONS = 4
N_ROW = 16
N_COL = 16


def draw_pair_count(key, part):
    key_density, key_spread, key_busiest = jax.random.split(key, 3)
    density = jax.random.randint(key_density, (N_ROW, N_COL, 1), 1, 9)
    spread = jax.random.randint(key_spread, (N_ROW, N_COL, SECTIONS), 5, 9)
    busiest = jax.random.randint(key_busiest, (), 0, N_ROW * N_COL)
    tile_ids = lax.iota(jnp.int32, N_ROW * N_COL).reshape(N_ROW, N_COL, 1)
    density = jnp.where(tile_ids == busiest, 8, density)
    first_section = jnp.where(tile_ids[:, :, 0] == busiest, 8, spread[:, :, 0])
    spread = spread.at[:, :, 0].set(first_section)
    return (PAIRS * density * spread // 64).astype(jnp.int32)


def plant(entries, key, low, top_value):
    longest = entries.shape.index(max(entries.shape))
    spots = []
    for shift in (0, 1):
        where = [jax.random.randint(jax.random.fold_in(key, axis), (), 0, length) for axis, length in enumerate(entries.shape)]
        where[longest] = (where[longest] + shift) % entries.shape[longest]
        spots.append(tuple(where))
    return entries.at[spots[0]].set(low).at[spots[1]].set(top_value)


def level_of(key, dims, pieces, smallest, top_value):
    def one(dim, blocks):
        heights = jax.random.uniform(jax.random.fold_in(jax.random.fold_in(key, 6), dim), (blocks,), jnp.float32, smallest / len(pieces), top_value / len(pieces))
        return jnp.repeat(jnp.exp(heights), dims[dim] // blocks).reshape((-1,) + (1,) * (len(dims) - dim - 1))

    level = one(*pieces[0])
    for cut in pieces[1:]:
        level = level * one(*cut)
    return level


def centred(rng, extent, width, limit, cuts=(), held_as=jnp.bfloat16):
    gain = level_of(rng, extent, cuts, -0.22, 0.18) if cuts else 1.0
    entries = jax.random.normal(rng, extent, jnp.float32) * width * gain
    return jnp.minimum(jnp.maximum(entries, -limit), limit).astype(held_as)


def setup_inputs(seed: int = 0) -> dict:
    streams_of = jax.random.split(jax.random.key(seed), 5)
    x_blocks = centred(streams_of[0], (N_ROW, N_COL, SLOTS, BLK, BLK), 0.15, 0.8984375, ((0, 16), (1, 16)))
    x_live = plant((jax.random.randint(streams_of[1], (N_ROW, N_COL, SLOTS), 0, 4) < 3).astype(jnp.int32), jax.random.fold_in(streams_of[1], 1), 0, 1)
    pair_slots = plant(jax.random.randint(streams_of[2], (N_ROW, N_COL, SECTIONS, 3, PAIRS), 0, SLOTS), jax.random.fold_in(streams_of[2], 1), 0, SLOTS - 1).astype(jnp.int32)
    pair_count = draw_pair_count(jax.random.fold_in(streams_of[4], 71), 0)
    return dict(x_blocks=x_blocks, x_live=x_live, pair_slots=pair_slots, pair_count=pair_count)


def add_pairs(gram_sum, left_piece, right_piece, picked, live_pairs):
    block_size = 48

    def one_block(block_no, running):
        first_pair = block_no * block_size
        chosen = lax.dynamic_slice_in_dim(picked, first_pair, block_size, 1)
        positions = first_pair + lax.iota(jnp.int32, block_size)
        weights = (positions < live_pairs).astype(jnp.float32)
        left_rows = jnp.take(left_piece, chosen[0], axis=0).astype(jnp.float32)
        right_rows = jnp.take(right_piece, chosen[1], axis=0).astype(jnp.float32)
        product = jnp.einsum("pik,pjk->pij", left_rows, right_rows)
        return running.at[chosen[2]].add(product * weights[:, None, None])

    return lax.fori_loop(0, picked.shape[1] // block_size, one_block, gram_sum)


def reference(x_blocks, x_live, pair_slots, pair_count):
    layers = N_ROW // N_COL
    filtered = x_blocks * x_live.astype(x_blocks.dtype)[:, :, :, None, None]

    def one_tile(tile_id):
        row_here = tile_id // N_COL
        col_here = tile_id % N_COL
        panel_here = row_here // layers
        within = row_here % layers
        gram_sum = jnp.zeros((SLOTS, BLK, BLK), jnp.float32)
        for section_no in range(SECTIONS):
            left_piece = filtered[row_here, (col_here + section_no) % N_COL]
            right_piece = filtered[col_here * layers + within, (panel_here + section_no) % N_COL]
            gram_sum = add_pairs(gram_sum, left_piece, right_piece, pair_slots[row_here, col_here, section_no], pair_count[row_here, col_here, section_no])
        return gram_sum

    all_grams = lax.map(one_tile, jnp.arange(N_ROW * N_COL, dtype=jnp.int32))
    return all_grams.reshape(N_ROW, N_COL, SLOTS, BLK, BLK)
```

```python
import functools

import jax
import jax.numpy as jnp
from jax import lax
from jax.experimental import pallas as pl
from jax.experimental.pallas import tpu as pltpu
from jax.sharding import PartitionSpec as P

SECTIONS = 4
SLOTS = 16
BLK = 128
PAIRS = 192
SIDE = 16
RING = 8
CHUNKS = 4
GROUP = 8
LISTED = 896
MESH = pl.DeviceIdType.MESH


def make_list(pairs, counts, left_live, right_live, listed, spans):
    slot_ids = lax.broadcasted_iota(jnp.int32, (SLOTS, PAIRS), 0)
    lanes = lax.broadcasted_iota(jnp.int32, (1, PAIRS), 1)
    earlier = (
        lax.broadcasted_iota(jnp.int32, (PAIRS, PAIRS), 0)
        < lax.broadcasted_iota(jnp.int32, (PAIRS, PAIRS), 1)
    ).astype(jnp.float32).astype(jnp.bfloat16)

    def hot(row):
        return (slot_ids == row).astype(jnp.float32)

    def look_up(live, row):
        table = jnp.broadcast_to(live.astype(jnp.float32), (8, SLOTS)).astype(jnp.bfloat16)
        return jnp.dot(
            table, hot(row).astype(jnp.bfloat16), preferred_element_type=jnp.float32
        )[0:1]

    chosen, places, totals = [], [], jnp.zeros((SLOTS, 1), jnp.float32)
    for s in range(SECTIONS):
        left, right, out = (pairs[s, k : k + 1, :] for k in range(3))
        used = look_up(left_live[s], left) * look_up(right_live[s], right)
        used = jnp.where(lanes < counts[s], used, 0.0)
        picked = hot(out) * used
        before = jnp.dot(picked.astype(jnp.bfloat16), earlier, preferred_element_type=jnp.float32)
        chosen.append(picked)
        places.append(before + totals)
        totals = totals + jnp.sum(picked, axis=1, keepdims=True)
    groups = jnp.floor((totals + (GROUP - 1)) * (1.0 / GROUP))
    below = (
        lax.broadcasted_iota(jnp.int32, (SLOTS, SLOTS), 1)
        < lax.broadcasted_iota(jnp.int32, (SLOTS, SLOTS), 0)
    ).astype(jnp.float32).astype(jnp.bfloat16)
    starts = jnp.dot(
        below,
        jnp.broadcast_to(groups, (SLOTS, BLK)).astype(jnp.bfloat16),
        preferred_element_type=jnp.float32,
    )
    lane = lax.broadcasted_iota(jnp.int32, (SLOTS, BLK), 1)
    spans[...] = jnp.where(lane == 0, starts, jnp.broadcast_to(groups, (SLOTS, BLK))).astype(jnp.int32)
    first = starts[:, 0:1] * GROUP
    gathered = jnp.zeros((8, LISTED), jnp.float32)
    positions = lax.broadcasted_iota(jnp.int32, (LISTED, PAIRS), 0).astype(jnp.float32)
    row_ids = lax.broadcasted_iota(jnp.int32, (8, PAIRS), 0)
    for s in range(SECTIONS):
        place = jnp.sum(chosen[s] * (places[s] + first + 1.0), axis=0, keepdims=True) - 1.0
        codes = jnp.where(row_ids == 0, pairs[s, 0:1, :], pairs[s, 1:2, :]) + (1 + SLOTS * s)
        gathered += lax.dot_general(
            codes.astype(jnp.float32).astype(jnp.bfloat16),
            (positions == place).astype(jnp.float32).astype(jnp.bfloat16),
            (((1,), (1,)), ((), ())),
            preferred_element_type=jnp.float32,
        )
    listed[...] = gathered.astype(jnp.int32)


def moves_kernel(
    x, live, pairs, counts, L, R, listed, spans,
    lv, rv, l_send, l_recv, r_send, r_recv, m_send, lv_send, lv_recv, rv_send, rv_recv, own_sem,
):
    a = lax.axis_index("row")
    b = lax.axis_index("col")

    def at(row, col):
        return (lax.rem(row + SIDE, SIDE), lax.rem(col + SIDE, SIDE))

    twin = a == b
    gap = lax.rem(lax.rem(b, RING) - lax.rem(a, RING) + RING, RING)
    back = lax.rem(RING - gap, RING)
    late = jnp.logical_or(back == 2, back == 3)
    step = jnp.where(late, 2, jnp.where(back == 1, 1, 0))
    out_0 = jnp.logical_or(gap == 0, gap >= 4)
    out_1 = gap == 0
    out_2 = gap <= 1
    not_twin = jnp.logical_not(twin)
    go_0 = jnp.logical_and(out_0, not_twin)

    barrier = pltpu.get_barrier_semaphore()

    def hello(device):
        pl.semaphore_signal(barrier, inc=1, device_id=device, device_id_type=MESH)

    hello(at(a, b + 1))
    hello(at(a + 1, b))
    hello(at(a + 2, b))

    @pl.when(not_twin)
    def _():
        hello(at(b, a))
        hello(at(b, a - step))

    one = jnp.int32(1)
    zero = jnp.int32(0)
    expected = (
        3
        + jnp.where(not_twin, one, zero)
        + jnp.where(go_0, one, zero)
        + jnp.where(out_1, one, zero)
        + jnp.where(out_2, one, zero)
    )
    pl.semaphore_wait(barrier, expected)

    size = SLOTS // CHUNKS

    def part(q):
        return pl.ds(q * size, size)

    def remote(src, dst, send, recv, device):
        return pltpu.make_async_remote_copy(
            src_ref=src, dst_ref=dst, send_sem=send, recv_sem=recv, device_id=device, device_id_type=MESH
        )

    def left(k, q):
        src = x.at[part(q)] if k == 0 else L.at[k - 1, part(q)]
        return remote(src, L.at[k, part(q)], l_send.at[k, q], l_recv.at[k, q], at(a, b - 1))

    def mirror(j, q):
        src = x.at[part(q)] if j == 0 else L.at[j - 1, part(q)]
        return remote(src, R.at[0, part(q)], m_send.at[j, q], r_recv.at[0, q], at(b + j, a))

    def right(k, q):
        src = R.at[2 if k == 3 else 0, part(q)]
        device = at(a - (2 if k == 2 else 1), b)
        return remote(src, R.at[k, part(q)], r_send.at[k, q], r_recv.at[k, q], device)

    def live_left(k):
        src = live if k == 0 else lv.at[k - 1]
        return remote(src, lv.at[k], lv_send.at[k], lv_recv.at[k], at(a, b - 1))

    def live_mirror(k):
        src = live if k == 0 else lv.at[k - 1]
        return remote(src, rv.at[k], rv_send.at[k], rv_recv.at[k], at(b, a))

    own = pltpu.make_async_copy(x, R.at[0], own_sem)

    live_left(0).start()

    @pl.when(not_twin)
    def _():
        live_mirror(0).start()

    @pl.when(twin)
    def _():
        own.start()

    for q in range(CHUNKS):
        left(0, q).start()

    @pl.when(go_0)
    def _():
        for q in range(CHUNKS):
            mirror(0, q).start()

    for k in range(3):
        live_left(k).wait_recv()
        if k < 2:
            live_left(k + 1).start()

        @pl.when(not_twin)
        def _():
            live_mirror(k + 1).start()

    @pl.when(not_twin)
    def _():
        for k in range(4):
            live_mirror(k).wait_recv()

    lefts = [live[...], lv[0], lv[1], lv[2]]
    rights = [jnp.where(twin, lefts[k], rv[k]) for k in range(4)]
    make_list(pairs, counts, lefts, rights, listed, spans)

    def take_mirror(q):
        @pl.when(not_twin)
        def _():
            mirror(0, q).wait_recv()

        right(1, q).start()
        right(2, q).start()

    def pass_on(q):
        right(2, q).wait_recv()
        right(3, q).start()

    for q in range(CHUNKS):
        left(0, q).wait_recv()
        left(1, q).start()

        @pl.when(out_1)
        def _():
            mirror(1, q).start()

    @pl.when(twin)
    def _():
        own.wait()

    for q in range(CHUNKS):
        @pl.when(late)
        def _():
            pass_on(q)

        @pl.when(jnp.logical_not(late))
        def _():
            take_mirror(q)

        left(1, q).wait_recv()
        left(2, q).start()

        @pl.when(out_2)
        def _():
            mirror(2, q).start()

    for q in range(CHUNKS):
        @pl.when(late)
        def _():
            take_mirror(q)

        @pl.when(jnp.logical_not(late))
        def _():
            pass_on(q)

    for q in range(CHUNKS):
        left(2, q).wait_recv()
        right(1, q).wait_recv()
        right(3, q).wait_recv()

    for q in range(CHUNKS):
        for k in range(3):
            left(k, q).wait_send()
            right(k + 1, q).wait_send()

        @pl.when(go_0)
        def _():
            mirror(0, q).wait_send()

        @pl.when(out_1)
        def _():
            mirror(1, q).wait_send()

        @pl.when(out_2)
        def _():
            mirror(2, q).wait_send()

    for k in range(3):
        live_left(k).wait_send()

    @pl.when(not_twin)
    def _():
        for k in range(4):
            live_mirror(k).wait_send()


def moves(x, live, pairs, counts):
    dma = pltpu.SemaphoreType.DMA
    tile = (SLOTS, BLK, BLK)
    return pl.pallas_call(
        moves_kernel,
        out_shape=[
            jax.ShapeDtypeStruct((3,) + tile, jnp.bfloat16),
            jax.ShapeDtypeStruct((4,) + tile, jnp.bfloat16),
            jax.ShapeDtypeStruct((8, LISTED), jnp.int32),
            jax.ShapeDtypeStruct((SLOTS, BLK), jnp.int32),
        ],
        in_specs=[
            pl.BlockSpec(memory_space=pl.ANY),
            pl.BlockSpec(memory_space=pltpu.VMEM),
            pl.BlockSpec(memory_space=pltpu.VMEM),
            pl.BlockSpec(memory_space=pltpu.SMEM),
        ],
        out_specs=[
            pl.BlockSpec(memory_space=pl.ANY),
            pl.BlockSpec(memory_space=pl.ANY),
            pl.BlockSpec(memory_space=pltpu.VMEM),
            pl.BlockSpec(memory_space=pltpu.VMEM),
        ],
        scratch_shapes=[
            pltpu.VMEM((3, 1, SLOTS), jnp.int32),
            pltpu.VMEM((4, 1, SLOTS), jnp.int32),
            dma((3, CHUNKS)), dma((3, CHUNKS)),
            dma((4, CHUNKS)), dma((4, CHUNKS)),
            dma((3, CHUNKS)),
            dma((3,)), dma((3,)), dma((4,)), dma((4,)),
            dma,
        ],
        compiler_params=pltpu.CompilerParams(collective_id=0, has_side_effects=True),
        name="moves",
    )(x, live, pairs, counts)


def sums_kernel(listed, spans, x, L, R, out, left, right, total, in_sems, out_sems):
    copies = [
        pltpu.make_async_copy(x, left.at[pl.ds(1, SLOTS)], in_sems.at[0]),
        pltpu.make_async_copy(L, left.at[pl.ds(1 + SLOTS, 3 * SLOTS)], in_sems.at[1]),
        pltpu.make_async_copy(R, right.at[pl.ds(1, 4 * SLOTS)], in_sems.at[2]),
    ]
    for c in copies:
        c.start()
    left[0] = jnp.zeros((BLK, BLK), jnp.bfloat16)
    right[0] = jnp.zeros((BLK, BLK), jnp.bfloat16)
    for c in copies:
        c.wait()

    def send(o):
        return pltpu.make_async_copy(total.at[o], out.at[o], out_sems.at[o])

    for o in range(SLOTS):
        start = spans[o, 0]

        def one_group(i, acc):
            base = (start + i) * GROUP
            for k in range(0, GROUP, 2):
                rows = jnp.concatenate([left[listed[0, base + k]], left[listed[0, base + k + 1]]], axis=1)
                cols = jnp.concatenate([right[listed[1, base + k]], right[listed[1, base + k + 1]]], axis=1)
                acc = acc + lax.dot_general(
                    rows, cols, (((1,), (1,)), ((), ())), preferred_element_type=jnp.float32
                )
            return acc

        total[o] = lax.fori_loop(0, spans[o, 1], one_group, jnp.zeros((BLK, BLK), jnp.float32))
        send(o).start()
    for o in range(SLOTS):
        send(o).wait()


def sums(listed, spans, x, L, R):
    return pl.pallas_call(
        sums_kernel,
        out_shape=jax.ShapeDtypeStruct((SLOTS, BLK, BLK), jnp.float32),
        in_specs=[pl.BlockSpec(memory_space=pltpu.SMEM)] * 2 + [pl.BlockSpec(memory_space=pl.ANY)] * 3,
        out_specs=pl.BlockSpec(memory_space=pl.ANY),
        scratch_shapes=[
            pltpu.VMEM((1 + 4 * SLOTS, BLK, BLK), jnp.bfloat16),
            pltpu.VMEM((1 + 4 * SLOTS, BLK, BLK), jnp.bfloat16),
            pltpu.VMEM((SLOTS, BLK, BLK), jnp.float32),
            pltpu.SemaphoreType.DMA((3,)),
            pltpu.SemaphoreType.DMA((SLOTS,)),
        ],
        name="sums",
    )(listed, spans, x, L, R)


def body(x_blocks, x_live, pair_slots, pair_count):
    x = x_blocks[0, 0]
    L, R, listed, spans = moves(x, x_live[0], pair_slots[0, 0], pair_count[0, 0])
    gram = sums(listed, spans, x, L.reshape(3 * SLOTS, BLK, BLK), R.reshape(4 * SLOTS, BLK, BLK))
    return gram[None, None]


def solution(mesh):
    return jax.shard_map(
        body,
        mesh=mesh,
        in_specs=(
            P("row", "col", None, None, None),
            P("row", "col", None),
            P("row", "col", None, None, None),
            P("row", "col", None),
        ),
        out_specs=P("row", "col", None, None, None),
        check_vma=False,
    )
```

```python
import functools

import jax
import jax.numpy as jnp
from jax import lax
from jax.experimental import pallas as pl
from jax.experimental.pallas import tpu as pltpu
from jax.sharding import PartitionSpec as P

SECTIONS = 4
SLOTS = 16
BLK = 128
PAIRS = 192
SIDE = 16
RING = 8
HALF = 8
CHUNKS = 4
NEAR = (0, 1, 2, 2, 0, 0, 0, 0)
GROUP = 4
LISTED = 896
GROUPS = 256
BATCH = 8
MESH = pl.DeviceIdType.MESH


def make_list(pairs, counts, left_live, right_live, listed, spans):
    slot_ids = lax.broadcasted_iota(jnp.int32, (SLOTS, PAIRS), 0)
    lanes = lax.broadcasted_iota(jnp.int32, (1, PAIRS), 1)
    earlier = (
        lax.broadcasted_iota(jnp.int32, (PAIRS, PAIRS), 0)
        < lax.broadcasted_iota(jnp.int32, (PAIRS, PAIRS), 1)
    ).astype(jnp.float32).astype(jnp.bfloat16)

    def hot(row):
        return (slot_ids == row).astype(jnp.float32)

    def look_up(live, row):
        table = jnp.broadcast_to(live.astype(jnp.float32), (8, SLOTS)).astype(jnp.bfloat16)
        return jnp.dot(
            table, hot(row).astype(jnp.bfloat16), preferred_element_type=jnp.float32
        )[0:1]

    chosen, places, totals = [], [], jnp.zeros((SLOTS, 1), jnp.float32)
    for s in range(SECTIONS):
        left, right, out = (pairs[k, s : s + 1, :] for k in range(3))
        used = look_up(left_live[s], left) * look_up(right_live[s], right)
        used = jnp.where(lanes < counts[s], used, 0.0)
        picked = hot(out) * used
        before = jnp.dot(picked.astype(jnp.bfloat16), earlier, preferred_element_type=jnp.float32)
        chosen.append(picked)
        places.append(before + totals)
        totals = totals + jnp.sum(picked, axis=1, keepdims=True)
    groups = jnp.floor((totals + (GROUP - 1)) * (1.0 / GROUP))
    below = (
        lax.broadcasted_iota(jnp.int32, (SLOTS, SLOTS), 1)
        < lax.broadcasted_iota(jnp.int32, (SLOTS, SLOTS), 0)
    ).astype(jnp.float32).astype(jnp.bfloat16)
    starts = jnp.dot(
        below,
        jnp.broadcast_to(groups, (SLOTS, BLK)).astype(jnp.bfloat16),
        preferred_element_type=jnp.float32,
    )
    lane = lax.broadcasted_iota(jnp.int32, (SLOTS, GROUPS), 1).astype(jnp.float32)
    slot = jnp.sum((lane >= starts[:, 0:1]).astype(jnp.float32), axis=0, keepdims=True) - 1.0
    total = jnp.sum(groups)
    spans[0:1, :] = jnp.where(lane[0:1] < total, slot, float(SLOTS)).astype(jnp.int32)
    spans[1:2, :] = jnp.full((1, GROUPS), total).astype(jnp.int32)
    first = starts[:, 0:1] * GROUP
    gathered = jnp.zeros((8, LISTED), jnp.float32)
    positions = lax.broadcasted_iota(jnp.int32, (LISTED, PAIRS), 0).astype(jnp.float32)
    row_ids = lax.broadcasted_iota(jnp.int32, (8, PAIRS), 0)
    for s in range(SECTIONS):
        place = jnp.sum(chosen[s] * (places[s] + first + 1.0), axis=0, keepdims=True) - 1.0
        codes = jnp.where(row_ids == 0, pairs[0, s : s + 1, :], pairs[1, s : s + 1, :]) + (1 + SLOTS * s)
        gathered += lax.dot_general(
            codes.astype(jnp.float32).astype(jnp.bfloat16),
            (positions == place).astype(jnp.float32).astype(jnp.bfloat16),
            (((1,), (1,)), ((), ())),
            preferred_element_type=jnp.float32,
        )
    listed[...] = gathered.astype(jnp.int32)


def moves_kernel(
    x, live, pairs, counts, L, R, X, Y, listed, spans,
    lv, rv, l_send, l_recv, r_send, r_recv, m_send, lv_send, lv_recv, rv_send, rv_recv, x_send, x_recv, y_send, y_recv, own_sem,
):
    a = lax.axis_index("row")
    b = lax.axis_index("col")

    def at(row, col):
        return (lax.rem(row + SIDE, SIDE), lax.rem(col + SIDE, SIDE))

    twin = a == b
    gap = lax.rem(lax.rem(b, RING) - lax.rem(a, RING) + RING, RING)
    back = lax.rem(RING - gap, RING)
    def any_of(value, options):
        found = value < 0
        for option in options:
            found = jnp.logical_or(found, value == option)
        return found

    late = any_of(back, [d for d in range(RING) if NEAR[d] >= 2])
    step = jnp.int32(0)
    for d in range(RING):
        step = jnp.where(back == d, NEAR[d], step)
    out_0, out_1, out_2 = (
        any_of(gap, [(d - j) % RING for d in range(RING) if NEAR[d] == j]) for j in range(3)
    )
    not_twin = jnp.logical_not(twin)
    go_0 = jnp.logical_and(out_0, not_twin)

    barrier = pltpu.get_barrier_semaphore()

    def hello(device):
        pl.semaphore_signal(barrier, inc=1, device_id=device, device_id_type=MESH)

    i = lax.rem(a, HALF)
    z = lax.rem(b, HALF)
    over_row = at(a + HALF, b)
    over_col = at(a, b + HALF)

    for k in range(1, 4):
        hello(at(a, b + k))
        hello(at(b, a + k))

    @pl.when(z == HALF - 1)
    def _():
        hello(at(a, b - HALF + 1))

    @pl.when(z == 0)
    def _():
        hello(over_col)

    for k in range(1, 4):
        hello(at(jnp.where(i + k >= HALF, a + k - HALF, a + k), b))

    @pl.when(i <= 2)
    def _():
        hello(over_row)

    @pl.when(not_twin)
    def _():
        hello(at(b, a))
        hello(at(b, a - step))

    one = jnp.int32(1)
    zero = jnp.int32(0)
    expected = (
        jnp.where(z == 0, jnp.int32(8), jnp.int32(6))
        + jnp.where(i <= 2, jnp.int32(4), jnp.int32(3))
        + jnp.where(not_twin, one, zero)
        + jnp.where(go_0, one, zero)
        + jnp.where(out_1, one, zero)
        + jnp.where(out_2, one, zero)
    )
    pl.semaphore_wait(barrier, expected)

    size = SLOTS // CHUNKS

    def part(q):
        return pl.ds(q * size, size)

    def remote(src, dst, send, recv, device):
        return pltpu.make_async_remote_copy(
            src_ref=src, dst_ref=dst, send_sem=send, recv_sem=recv, device_id=device, device_id_type=MESH
        )

    def left_src(k, q):
        return x.at[part(q)] if k == 0 else L.at[k - 1, part(q)]

    def left(k, q):
        return remote(left_src(k, q), L.at[k, part(q)], l_send.at[k, q], l_recv.at[k, q], at(a, b - 1))

    def left_over(k, q):
        return remote(left_src(k, q), Y.at[k, part(q)], l_send.at[k, q], y_recv.at[k, q], over_col)

    def left_after(k, q):
        return remote(Y.at[k, part(q)], L.at[k, part(q)], y_send.at[k, q], l_recv.at[k, q], at(a, b + HALF - 1))

    def start_left(k, q):
        if q % 2 == 0:
            left(k, q).start()
        else:
            @pl.when(z == 0)
            def _():
                left_over(k, q).start()

            @pl.when(z != 0)
            def _():
                left(k, q).start()

    def cross_left(k, q):
        if q % 2 == 1:
            @pl.when(z == 0)
            def _():
                left_over(k, q).wait_recv()
                left_after(k, q).start()

    def mirror(j, q):
        src = x.at[part(q)] if j == 0 else L.at[j - 1, part(q)]
        return remote(src, R.at[0, part(q)], m_send.at[j, q], r_recv.at[0, q], at(b + j, a))

    def right(k, q):
        return remote(R.at[0, part(q)], R.at[k, part(q)], r_send.at[k, q], r_recv.at[k, q], at(a - k, b))

    def right_over(q):
        return remote(R.at[0, part(q)], X.at[part(q)], x_send.at[3, q], x_recv.at[q], over_row)

    def right_after(k, q):
        return remote(X.at[part(q)], R.at[k, part(q)], x_send.at[k - 1, q], r_recv.at[k, q], at(a + HALF - k, b))

    def live_left(k):
        return remote(live, lv.at[k], lv_send.at[k], lv_recv.at[k], at(a, b - 1 - k))

    def live_mirror(k):
        return remote(live, rv.at[k], rv_send.at[k], rv_recv.at[k], at(b - k, a))

    own = pltpu.make_async_copy(x, R.at[0], own_sem)

    for k in range(3):
        live_left(k).start()
        live_mirror(k + 1).start()

    @pl.when(not_twin)
    def _():
        live_mirror(0).start()

    @pl.when(twin)
    def _():
        own.start()

    for q in range(CHUNKS):
        @pl.when(go_0)
        def _():
            mirror(0, q).start()

        start_left(0, q)

    def take_mirror(q):
        @pl.when(not_twin)
        def _():
            mirror(0, q).wait_recv()

        @pl.when(i <= 2)
        def _():
            right_over(q).start()

        for k in range(1, 4):
            @pl.when(i >= k)
            def _():
                right(k, q).start()

    def cross_right(q):
        @pl.when(i <= 2)
        def _():
            right_over(q).wait_recv()

            for k in range(1, 4):
                @pl.when(i < k)
                def _():
                    right_after(k, q).start()

    def take_and_cross(q):
        take_mirror(q)
        if q > 0:
            cross_right(q - 1)
        if q == CHUNKS - 1:
            cross_right(q)

    for q in range(CHUNKS):
        if q > 0:
            cross_left(0, q - 1)
        left(0, q).wait_recv()

        @pl.when(out_1)
        def _():
            mirror(1, q).start()

        start_left(1, q)
    cross_left(0, CHUNKS - 1)

    for k in range(3):
        live_left(k).wait_recv()
        live_mirror(k + 1).wait_recv()

    @pl.when(not_twin)
    def _():
        live_mirror(0).wait_recv()

    lefts = [live[...], lv[0], lv[1], lv[2]]
    rights = [jnp.where(twin, live[...], rv[0]), rv[1], rv[2], rv[3]]
    make_list(pairs, counts, lefts, rights, listed, spans)

    @pl.when(twin)
    def _():
        own.wait()

    for q in range(CHUNKS):
        cross_left(1, q)

        @pl.when(jnp.logical_not(late))
        def _():
            take_and_cross(q)

        left(1, q).wait_recv()

        @pl.when(out_2)
        def _():
            mirror(2, q).start()

        start_left(2, q)

    for q in range(CHUNKS):
        cross_left(2, q)

        @pl.when(late)
        def _():
            take_and_cross(q)

    for q in range(CHUNKS):
        left(2, q).wait_recv()
        for k in range(1, 4):
            right(k, q).wait_recv()

    for q in range(CHUNKS):
        for k in range(3):
            left(k, q).wait_send()
            if q % 2 == 1:
                @pl.when(z == 0)
                def _():
                    left_after(k, q).wait_send()

        for k in range(1, 4):
            @pl.when(i >= k)
            def _():
                right(k, q).wait_send()

            @pl.when(i < k)
            def _():
                right_after(k, q).wait_send()

        @pl.when(i <= 2)
        def _():
            right_over(q).wait_send()

        @pl.when(go_0)
        def _():
            mirror(0, q).wait_send()

        @pl.when(out_1)
        def _():
            mirror(1, q).wait_send()

        @pl.when(out_2)
        def _():
            mirror(2, q).wait_send()

    for k in range(3):
        live_left(k).wait_send()
        live_mirror(k + 1).wait_send()

    @pl.when(not_twin)
    def _():
        live_mirror(0).wait_send()


def moves(x, live, pairs, counts):
    dma = pltpu.SemaphoreType.DMA
    tile = (SLOTS, BLK, BLK)
    return pl.pallas_call(
        moves_kernel,
        out_shape=[
            jax.ShapeDtypeStruct((3,) + tile, jnp.bfloat16),
            jax.ShapeDtypeStruct((4,) + tile, jnp.bfloat16),
            jax.ShapeDtypeStruct(tile, jnp.bfloat16),
            jax.ShapeDtypeStruct((3,) + tile, jnp.bfloat16),
            jax.ShapeDtypeStruct((8, LISTED), jnp.int32),
            jax.ShapeDtypeStruct((8, GROUPS), jnp.int32),
        ],
        in_specs=[
            pl.BlockSpec(memory_space=pl.ANY),
            pl.BlockSpec(memory_space=pltpu.VMEM),
            pl.BlockSpec(memory_space=pltpu.VMEM),
            pl.BlockSpec(memory_space=pltpu.SMEM),
        ],
        out_specs=[
            pl.BlockSpec(memory_space=pl.ANY),
            pl.BlockSpec(memory_space=pl.ANY),
            pl.BlockSpec(memory_space=pl.ANY),
            pl.BlockSpec(memory_space=pl.ANY),
            pl.BlockSpec(memory_space=pltpu.VMEM),
            pl.BlockSpec(memory_space=pltpu.VMEM),
        ],
        scratch_shapes=[
            pltpu.VMEM((3, 1, SLOTS), jnp.int32),
            pltpu.VMEM((4, 1, SLOTS), jnp.int32),
            dma((3, CHUNKS)), dma((3, CHUNKS)),
            dma((4, CHUNKS)), dma((4, CHUNKS)),
            dma((3, CHUNKS)),
            dma((3,)), dma((3,)), dma((4,)), dma((4,)),
            dma((4, CHUNKS)), dma((CHUNKS,)), dma((3, CHUNKS)), dma((3, CHUNKS)),
            dma,
        ],
        compiler_params=pltpu.CompilerParams(collective_id=0, has_side_effects=True),
        name="moves",
    )(x, live, pairs, counts)


def sums_kernel(listed, spans, x, L, R, out, left, right, total, in_sems, out_sem):
    copies = [
        pltpu.make_async_copy(x, left.at[pl.ds(1, SLOTS)], in_sems.at[0]),
        pltpu.make_async_copy(L, left.at[pl.ds(1 + SLOTS, 3 * SLOTS)], in_sems.at[1]),
        pltpu.make_async_copy(R, right.at[pl.ds(1, 4 * SLOTS)], in_sems.at[2]),
    ]
    for c in copies:
        c.start()
    left[0] = jnp.zeros((BLK, BLK), jnp.bfloat16)
    right[0] = jnp.zeros((BLK, BLK), jnp.bfloat16)
    for c in copies:
        c.wait()

    for o in range(SLOTS):
        total[o] = jnp.zeros((BLK, BLK), jnp.float32)

    def batch(i, carry):
        for u in range(BATCH):
            group = i * BATCH + u
            base = group * GROUP
            product = None
            for k in range(0, GROUP, GROUP):
                rows = jnp.concatenate([left[listed[0, base + n]] for n in range(GROUP)], axis=1)
                cols = jnp.concatenate([right[listed[1, base + n]] for n in range(GROUP)], axis=1)
                term = lax.dot_general(
                    rows, cols, (((1,), (1,)), ((), ())), preferred_element_type=jnp.float32
                )
                product = term if product is None else product + term
            total[spans[0, group]] += product
        return carry

    lax.fori_loop(0, lax.div(spans[1, 0] + (BATCH - 1), BATCH), batch, 0)
    done = pltpu.make_async_copy(total.at[pl.ds(0, SLOTS)], out, out_sem)
    done.start()
    done.wait()


def sums(listed, spans, x, L, R):
    return pl.pallas_call(
        sums_kernel,
        out_shape=jax.ShapeDtypeStruct((SLOTS, BLK, BLK), jnp.float32),
        in_specs=[pl.BlockSpec(memory_space=pltpu.SMEM)] * 2 + [pl.BlockSpec(memory_space=pl.ANY)] * 3,
        out_specs=pl.BlockSpec(memory_space=pl.ANY),
        scratch_shapes=[
            pltpu.VMEM((1 + 4 * SLOTS, BLK, BLK), jnp.bfloat16),
            pltpu.VMEM((1 + 4 * SLOTS, BLK, BLK), jnp.bfloat16),
            pltpu.VMEM((SLOTS + 1, BLK, BLK), jnp.float32),
            pltpu.SemaphoreType.DMA((3,)),
            pltpu.SemaphoreType.DMA,
        ],
        name="sums",
    )(listed, spans, x, L, R)


def body(x_blocks, x_live, pair_slots, pair_count):
    x = x_blocks[0, 0]
    L, R, _, _, listed, spans = moves(x, x_live[0], jnp.swapaxes(pair_slots[0, 0], 0, 1), pair_count[0, 0])
    gram = sums(listed, spans, x, L.reshape(3 * SLOTS, BLK, BLK), R.reshape(4 * SLOTS, BLK, BLK))
    return gram[None, None]


def solution(mesh):
    return jax.shard_map(
        body,
        mesh=mesh,
        in_specs=(
            P("row", "col", None, None, None),
            P("row", "col", None),
            P("row", "col", None, None, None),
            P("row", "col", None),
        ),
        out_specs=P("row", "col", None, None, None),
        check_vma=False,
    )
```

```python
import functools

import jax
import jax.numpy as jnp
from jax import lax
from jax.experimental import pallas as pl
from jax.experimental.pallas import tpu as pltpu
from jax.sharding import PartitionSpec as P

SECTIONS = 4
SLOTS = 16
BLK = 128
PAIRS = 192
SIDE = 16
RING = 8
HALF = 8
CHUNKS = 4
NEAR = (0, 1, 2, 1, 0, 0, 0, 0)
GROUP = 4
LISTED = 896
GROUPS = 256
BATCH = 16
MESH = pl.DeviceIdType.MESH


def make_list(pairs, counts, left_live, right_live, listed, spans):
    slot_ids = lax.broadcasted_iota(jnp.int32, (SLOTS, PAIRS), 0)
    lanes = lax.broadcasted_iota(jnp.int32, (1, PAIRS), 1)
    earlier = (
        lax.broadcasted_iota(jnp.int32, (PAIRS, PAIRS), 0)
        < lax.broadcasted_iota(jnp.int32, (PAIRS, PAIRS), 1)
    ).astype(jnp.float32).astype(jnp.bfloat16)

    def hot(row):
        return (slot_ids == row).astype(jnp.float32)

    def look_up(live, row):
        table = jnp.broadcast_to(live.astype(jnp.float32), (8, SLOTS)).astype(jnp.bfloat16)
        return jnp.dot(
            table, hot(row).astype(jnp.bfloat16), preferred_element_type=jnp.float32
        )[0:1]

    chosen, places, totals = [], [], jnp.zeros((SLOTS, 1), jnp.float32)
    for s in range(SECTIONS):
        left, right, out = (pairs[k, s : s + 1, :] for k in range(3))
        used = look_up(left_live[s], left) * look_up(right_live[s], right)
        used = jnp.where(lanes < counts[s], used, 0.0)
        picked = hot(out) * used
        before = jnp.dot(picked.astype(jnp.bfloat16), earlier, preferred_element_type=jnp.float32)
        chosen.append(picked)
        places.append(before + totals)
        totals = totals + jnp.sum(picked, axis=1, keepdims=True)
    groups = jnp.floor((totals + (GROUP - 1)) * (1.0 / GROUP))
    below = (
        lax.broadcasted_iota(jnp.int32, (SLOTS, SLOTS), 1)
        < lax.broadcasted_iota(jnp.int32, (SLOTS, SLOTS), 0)
    ).astype(jnp.float32).astype(jnp.bfloat16)
    starts = jnp.dot(
        below,
        jnp.broadcast_to(groups, (SLOTS, BLK)).astype(jnp.bfloat16),
        preferred_element_type=jnp.float32,
    )
    lane = lax.broadcasted_iota(jnp.int32, (SLOTS, GROUPS), 1).astype(jnp.float32)
    slot = jnp.sum((lane >= starts[:, 0:1]).astype(jnp.float32), axis=0, keepdims=True) - 1.0
    total = jnp.sum(groups)
    spans[0:1, :] = jnp.where(lane[0:1] < total, slot, float(SLOTS)).astype(jnp.int32)
    spans[1:2, :] = jnp.full((1, GROUPS), total).astype(jnp.int32)
    first = starts[:, 0:1] * GROUP
    gathered = jnp.zeros((8, LISTED), jnp.float32)
    positions = lax.broadcasted_iota(jnp.int32, (LISTED, PAIRS), 0).astype(jnp.float32)
    row_ids = lax.broadcasted_iota(jnp.int32, (8, PAIRS), 0)
    for s in range(SECTIONS):
        place = jnp.sum(chosen[s] * (places[s] + first + 1.0), axis=0, keepdims=True) - 1.0
        codes = jnp.where(row_ids == 0, pairs[0, s : s + 1, :], pairs[1, s : s + 1, :]) + (1 + SLOTS * s)
        gathered += lax.dot_general(
            codes.astype(jnp.float32).astype(jnp.bfloat16),
            (positions == place).astype(jnp.float32).astype(jnp.bfloat16),
            (((1,), (1,)), ((), ())),
            preferred_element_type=jnp.float32,
        )
    listed[...] = gathered.astype(jnp.int32)


def moves_kernel(
    x, live, pairs, counts, L, R, X, Y, listed, spans,
    lv, rv, l_send, l_recv, r_send, r_recv, m_send, lv_send, lv_recv, rv_send, rv_recv, x_send, x_recv, y_send, y_recv, h_send, own_sem,
):
    a = lax.axis_index("row")
    b = lax.axis_index("col")

    def at(row, col):
        return (lax.rem(row + SIDE, SIDE), lax.rem(col + SIDE, SIDE))

    twin = a == b
    gap = lax.rem(lax.rem(b, RING) - lax.rem(a, RING) + RING, RING)
    back = lax.rem(RING - gap, RING)
    def any_of(value, options):
        found = value < 0
        for option in options:
            found = jnp.logical_or(found, value == option)
        return found

    late = any_of(back, [d for d in range(RING) if NEAR[d] >= 2])
    step = jnp.int32(0)
    for d in range(RING):
        step = jnp.where(back == d, NEAR[d], step)
    out_0, out_1, out_2 = (
        any_of(gap, [(d - j) % RING for d in range(RING) if NEAR[d] == j]) for j in range(3)
    )
    not_twin = jnp.logical_not(twin)
    go_0 = jnp.logical_and(out_0, not_twin)

    barrier = pltpu.get_barrier_semaphore()

    def hello(device):
        pl.semaphore_signal(barrier, inc=1, device_id=device, device_id_type=MESH)

    i = lax.rem(a, HALF)
    z = lax.rem(b, HALF)
    over_row = at(a + HALF, b)
    over_col = at(a, b + HALF)

    for k in range(1, 4):
        hello(at(a, b + k))
        hello(at(b, a + k))

    @pl.when(z == HALF - 1)
    def _():
        hello(at(a, b - HALF + 1))

    @pl.when(z == 0)
    def _():
        hello(over_col)

    odd = lax.rem(a, 2) == 1
    hello(at(jnp.where(i + 1 >= HALF, a + 1 - HALF, a + 1), b))

    @pl.when(odd)
    def _():
        for k in range(2, 4):
            hello(at(jnp.where(i + k >= HALF, a + k - HALF, a + k), b))

    @pl.when(i <= 2)
    def _():
        hello(over_row)

    @pl.when(not_twin)
    def _():
        hello(at(b, a))
        hello(at(b, a - step))

    one = jnp.int32(1)
    zero = jnp.int32(0)
    expected = (
        jnp.where(z == 0, jnp.int32(8), jnp.int32(6))
        + jnp.where(i <= 2, jnp.int32(3), jnp.int32(2))
        + jnp.where(not_twin, one, zero)
        + jnp.where(go_0, one, zero)
        + jnp.where(out_1, one, zero)
        + jnp.where(out_2, one, zero)
    )
    pl.semaphore_wait(barrier, expected)

    size = SLOTS // CHUNKS

    def part(q):
        return pl.ds(q * size, size)

    def remote(src, dst, send, recv, device):
        return pltpu.make_async_remote_copy(
            src_ref=src, dst_ref=dst, send_sem=send, recv_sem=recv, device_id=device, device_id_type=MESH
        )

    def left_src(k, q):
        return x.at[part(q)] if k == 0 else L.at[k - 1, part(q)]

    def left(k, q):
        return remote(left_src(k, q), L.at[k, part(q)], l_send.at[k, q], l_recv.at[k, q], at(a, b - 1))

    def left_over(k, q):
        return remote(left_src(k, q), Y.at[k, part(q)], l_send.at[k, q], y_recv.at[k, q], over_col)

    def left_after(k, q):
        return remote(Y.at[k, part(q)], L.at[k, part(q)], y_send.at[k, q], l_recv.at[k, q], at(a, b + HALF - 1))

    def start_left(k, q):
        if q % 2 == 0:
            left(k, q).start()
        else:
            @pl.when(z == 0)
            def _():
                left_over(k, q).start()

            @pl.when(z != 0)
            def _():
                left(k, q).start()

    def cross_left(k, q):
        if q % 2 == 1:
            @pl.when(z == 0)
            def _():
                left_over(k, q).wait_recv()
                left_after(k, q).start()

    def mirror(j, q):
        src = x.at[part(q)] if j == 0 else L.at[j - 1, part(q)]
        return remote(src, R.at[0, part(q)], m_send.at[j, q], r_recv.at[0, q], at(b + j, a))

    def right(k, q):
        return remote(R.at[0, part(q)], R.at[k, part(q)], r_send.at[k, q], r_recv.at[k, q], at(a - k, b))

    def hand_on(k, q):
        return remote(R.at[k - 1, part(q)], R.at[k, part(q)], h_send.at[k - 2, q], r_recv.at[k, q], at(a - 1, b))

    def to_row(k, here):
        return here if k == 1 else jnp.logical_and(here, odd if k == 2 else jnp.logical_not(odd))

    def right_over(q):
        return remote(R.at[0, part(q)], X.at[part(q)], x_send.at[3, q], x_recv.at[q], over_row)

    def right_after(k, q):
        return remote(X.at[part(q)], R.at[k, part(q)], x_send.at[k - 1, q], r_recv.at[k, q], at(a + HALF - k, b))

    def live_left(k):
        return remote(live, lv.at[k], lv_send.at[k], lv_recv.at[k], at(a, b - 1 - k))

    def live_mirror(k):
        return remote(live, rv.at[k], rv_send.at[k], rv_recv.at[k], at(b - k, a))

    own = pltpu.make_async_copy(x, R.at[0], own_sem)

    for k in range(3):
        live_left(k).start()
        live_mirror(k + 1).start()

    @pl.when(not_twin)
    def _():
        live_mirror(0).start()

    @pl.when(twin)
    def _():
        own.start()

    for q in range(CHUNKS):
        @pl.when(go_0)
        def _():
            mirror(0, q).start()

        start_left(0, q)

    def take_mirror(q):
        @pl.when(not_twin)
        def _():
            mirror(0, q).wait_recv()

        @pl.when(i <= 2)
        def _():
            right_over(q).start()

        for k in range(1, 4):
            @pl.when(to_row(k, i >= k))
            def _():
                right(k, q).start()

    def cross_right(q):
        @pl.when(i <= 2)
        def _():
            right_over(q).wait_recv()

            for k in range(1, 4):
                @pl.when(to_row(k, i < k))
                def _():
                    right_after(k, q).start()

    def take_and_cross(q):
        take_mirror(q)
        if q > 0:
            cross_right(q - 1)
        if q == CHUNKS - 1:
            cross_right(q)

    for q in range(CHUNKS):
        if q > 0:
            cross_left(0, q - 1)
        left(0, q).wait_recv()

        @pl.when(out_1)
        def _():
            mirror(1, q).start()

        start_left(1, q)
    cross_left(0, CHUNKS - 1)

    for k in range(3):
        live_left(k).wait_recv()
        live_mirror(k + 1).wait_recv()

    @pl.when(not_twin)
    def _():
        live_mirror(0).wait_recv()

    lefts = [live[...], lv[0], lv[1], lv[2]]
    rights = [jnp.where(twin, live[...], rv[0]), rv[1], rv[2], rv[3]]
    make_list(pairs, counts, lefts, rights, listed, spans)

    @pl.when(twin)
    def _():
        own.wait()

    for q in range(CHUNKS):
        cross_left(1, q)

        @pl.when(jnp.logical_not(late))
        def _():
            take_and_cross(q)

        left(1, q).wait_recv()

        @pl.when(out_2)
        def _():
            mirror(2, q).start()

        start_left(2, q)

    for q in range(CHUNKS):
        cross_left(2, q)

        @pl.when(late)
        def _():
            take_and_cross(q)

    for q in range(CHUNKS):
        for k in range(1, 4):
            right(k, q).wait_recv()
            if k < 3:
                @pl.when(odd)
                def _():
                    hand_on(k + 1, q).start()

    for q in range(CHUNKS):
        left(2, q).wait_recv()

        @pl.when(odd)
        def _():
            hand_on(2, q).wait_send()
            hand_on(3, q).wait_send()

    for q in range(CHUNKS):
        for k in range(3):
            left(k, q).wait_send()
            if q % 2 == 1:
                @pl.when(z == 0)
                def _():
                    left_after(k, q).wait_send()

        for k in range(1, 4):
            @pl.when(to_row(k, i >= k))
            def _():
                right(k, q).wait_send()

            @pl.when(to_row(k, i < k))
            def _():
                right_after(k, q).wait_send()

        @pl.when(i <= 2)
        def _():
            right_over(q).wait_send()

        @pl.when(go_0)
        def _():
            mirror(0, q).wait_send()

        @pl.when(out_1)
        def _():
            mirror(1, q).wait_send()

        @pl.when(out_2)
        def _():
            mirror(2, q).wait_send()

    for k in range(3):
        live_left(k).wait_send()
        live_mirror(k + 1).wait_send()

    @pl.when(not_twin)
    def _():
        live_mirror(0).wait_send()


def moves(x, live, pairs, counts):
    dma = pltpu.SemaphoreType.DMA
    tile = (SLOTS, BLK, BLK)
    return pl.pallas_call(
        moves_kernel,
        out_shape=[
            jax.ShapeDtypeStruct((3,) + tile, jnp.bfloat16),
            jax.ShapeDtypeStruct((4,) + tile, jnp.bfloat16),
            jax.ShapeDtypeStruct(tile, jnp.bfloat16),
            jax.ShapeDtypeStruct((3,) + tile, jnp.bfloat16),
            jax.ShapeDtypeStruct((8, LISTED), jnp.int32),
            jax.ShapeDtypeStruct((8, GROUPS), jnp.int32),
        ],
        in_specs=[
            pl.BlockSpec(memory_space=pl.ANY),
            pl.BlockSpec(memory_space=pltpu.VMEM),
            pl.BlockSpec(memory_space=pltpu.VMEM),
            pl.BlockSpec(memory_space=pltpu.SMEM),
        ],
        out_specs=[
            pl.BlockSpec(memory_space=pl.ANY),
            pl.BlockSpec(memory_space=pl.ANY),
            pl.BlockSpec(memory_space=pl.ANY),
            pl.BlockSpec(memory_space=pl.ANY),
            pl.BlockSpec(memory_space=pltpu.VMEM),
            pl.BlockSpec(memory_space=pltpu.VMEM),
        ],
        scratch_shapes=[
            pltpu.VMEM((3, 1, SLOTS), jnp.int32),
            pltpu.VMEM((4, 1, SLOTS), jnp.int32),
            dma((3, CHUNKS)), dma((3, CHUNKS)),
            dma((4, CHUNKS)), dma((4, CHUNKS)),
            dma((3, CHUNKS)),
            dma((3,)), dma((3,)), dma((4,)), dma((4,)),
            dma((4, CHUNKS)), dma((CHUNKS,)), dma((3, CHUNKS)), dma((3, CHUNKS)),
            dma((2, CHUNKS)),
            dma,
        ],
        compiler_params=pltpu.CompilerParams(collective_id=0, has_side_effects=True),
        name="moves",
    )(x, live, pairs, counts)


def sums_kernel(listed, spans, x, L, R, out, left, right, total, in_sems, out_sem):
    copies = [
        pltpu.make_async_copy(x, left.at[pl.ds(1, SLOTS)], in_sems.at[0]),
        pltpu.make_async_copy(L, left.at[pl.ds(1 + SLOTS, 3 * SLOTS)], in_sems.at[1]),
        pltpu.make_async_copy(R, right.at[pl.ds(1, 4 * SLOTS)], in_sems.at[2]),
    ]
    for c in copies:
        c.start()
    left[0] = jnp.zeros((BLK, BLK), jnp.bfloat16)
    right[0] = jnp.zeros((BLK, BLK), jnp.bfloat16)
    for c in copies:
        c.wait()

    for o in range(SLOTS):
        total[o] = jnp.zeros((BLK, BLK), jnp.float32)

    def batch(i, carry):
        for u in range(BATCH):
            group = i * BATCH + u
            base = group * GROUP
            product = None
            for k in range(0, GROUP, GROUP):
                rows = jnp.concatenate([left[listed[0, base + n]] for n in range(GROUP)], axis=1)
                cols = jnp.concatenate([right[listed[1, base + n]] for n in range(GROUP)], axis=1)
                term = lax.dot_general(
                    rows, cols, (((1,), (1,)), ((), ())), preferred_element_type=jnp.float32
                )
                product = term if product is None else product + term
            total[spans[0, group]] += product
        return carry

    lax.fori_loop(0, lax.div(spans[1, 0] + (BATCH - 1), BATCH), batch, 0)
    done = pltpu.make_async_copy(total.at[pl.ds(0, SLOTS)], out, out_sem)
    done.start()
    done.wait()


def sums(listed, spans, x, L, R):
    return pl.pallas_call(
        sums_kernel,
        out_shape=jax.ShapeDtypeStruct((SLOTS, BLK, BLK), jnp.float32),
        in_specs=[pl.BlockSpec(memory_space=pltpu.SMEM)] * 2 + [pl.BlockSpec(memory_space=pl.ANY)] * 3,
        out_specs=pl.BlockSpec(memory_space=pl.ANY),
        scratch_shapes=[
            pltpu.VMEM((1 + 4 * SLOTS, BLK, BLK), jnp.bfloat16),
            pltpu.VMEM((1 + 4 * SLOTS, BLK, BLK), jnp.bfloat16),
            pltpu.VMEM((SLOTS + 1, BLK, BLK), jnp.float32),
            pltpu.SemaphoreType.DMA((3,)),
            pltpu.SemaphoreType.DMA,
        ],
        name="sums",
    )(listed, spans, x, L, R)


def body(x_blocks, x_live, pair_slots, pair_count):
    x = x_blocks[0, 0]
    L, R, _, _, listed, spans = moves(x, x_live[0], jnp.swapaxes(pair_slots[0, 0], 0, 1), pair_count[0, 0])
    gram = sums(listed, spans, x, L.reshape(3 * SLOTS, BLK, BLK), R.reshape(4 * SLOTS, BLK, BLK))
    return gram[None, None]


def solution(mesh):
    return jax.shard_map(
        body,
        mesh=mesh,
        in_specs=(
            P("row", "col", None, None, None),
            P("row", "col", None),
            P("row", "col", None, None, None),
            P("row", "col", None),
        ),
        out_specs=P("row", "col", None, None, None),
        check_vma=False,
    )
```

```python
import functools

import jax
import jax.numpy as jnp
from jax import lax
from jax.experimental import pallas as pl
from jax.experimental.pallas import tpu as pltpu
from jax.sharding import PartitionSpec as P

SECTIONS = 4
SLOTS = 16
BLK = 128
PAIRS = 192
SIDE = 16
RING = 8
HALF = 8
CHUNKS = 8
NEAR = (0, 1, 2, 1, 0, 0, 0, 0)
GROUP = 4
LISTED = 896
GROUPS = 256
BATCH = 16
MESH = pl.DeviceIdType.MESH


def make_list(pairs, counts, left_live, right_live, listed, spans):
    slot_ids = lax.broadcasted_iota(jnp.int32, (SLOTS, PAIRS), 0)
    lanes = lax.broadcasted_iota(jnp.int32, (1, PAIRS), 1)
    earlier = (
        lax.broadcasted_iota(jnp.int32, (PAIRS, PAIRS), 0)
        < lax.broadcasted_iota(jnp.int32, (PAIRS, PAIRS), 1)
    ).astype(jnp.float32).astype(jnp.bfloat16)

    def hot(row):
        return (slot_ids == row).astype(jnp.float32)

    def look_up(live, row):
        table = jnp.broadcast_to(live.astype(jnp.float32), (8, SLOTS)).astype(jnp.bfloat16)
        return jnp.dot(
            table, hot(row).astype(jnp.bfloat16), preferred_element_type=jnp.float32
        )[0:1]

    chosen, places, totals = [], [], jnp.zeros((SLOTS, 1), jnp.float32)
    for s in range(SECTIONS):
        left, right, out = (pairs[k, s : s + 1, :] for k in range(3))
        used = look_up(left_live[s], left) * look_up(right_live[s], right)
        used = jnp.where(lanes < counts[s], used, 0.0)
        picked = hot(out) * used
        before = jnp.dot(picked.astype(jnp.bfloat16), earlier, preferred_element_type=jnp.float32)
        chosen.append(picked)
        places.append(before + totals)
        totals = totals + jnp.sum(picked, axis=1, keepdims=True)
    groups = jnp.floor((totals + (GROUP - 1)) * (1.0 / GROUP))
    below = (
        lax.broadcasted_iota(jnp.int32, (SLOTS, SLOTS), 1)
        < lax.broadcasted_iota(jnp.int32, (SLOTS, SLOTS), 0)
    ).astype(jnp.float32).astype(jnp.bfloat16)
    starts = jnp.dot(
        below,
        jnp.broadcast_to(groups, (SLOTS, BLK)).astype(jnp.bfloat16),
        preferred_element_type=jnp.float32,
    )
    lane = lax.broadcasted_iota(jnp.int32, (SLOTS, GROUPS), 1).astype(jnp.float32)
    slot = jnp.sum((lane >= starts[:, 0:1]).astype(jnp.float32), axis=0, keepdims=True) - 1.0
    total = jnp.sum(groups)
    spans[0:1, :] = jnp.where(lane[0:1] < total, slot, float(SLOTS)).astype(jnp.int32)
    spans[1:2, :] = jnp.full((1, GROUPS), total).astype(jnp.int32)
    first = starts[:, 0:1] * GROUP
    gathered = jnp.zeros((8, LISTED), jnp.float32)
    positions = lax.broadcasted_iota(jnp.int32, (LISTED, PAIRS), 0).astype(jnp.float32)
    row_ids = lax.broadcasted_iota(jnp.int32, (8, PAIRS), 0)
    for s in range(SECTIONS):
        place = jnp.sum(chosen[s] * (places[s] + first + 1.0), axis=0, keepdims=True) - 1.0
        codes = jnp.where(row_ids == 0, pairs[0, s : s + 1, :], pairs[1, s : s + 1, :]) + (1 + SLOTS * s)
        gathered += lax.dot_general(
            codes.astype(jnp.float32).astype(jnp.bfloat16),
            (positions == place).astype(jnp.float32).astype(jnp.bfloat16),
            (((1,), (1,)), ((), ())),
            preferred_element_type=jnp.float32,
        )
    listed[...] = gathered.astype(jnp.int32)


def moves_kernel(
    x, live, pairs, counts, L, R, X, Y, listed, spans,
    lv, rv, l_send, l_recv, r_send, r_recv, m_send, lv_send, lv_recv, rv_send, rv_recv, x_send, x_recv, y_send, y_recv, h_send, own_sem,
):
    a = lax.axis_index("row")
    b = lax.axis_index("col")

    def at(row, col):
        return (lax.rem(row + SIDE, SIDE), lax.rem(col + SIDE, SIDE))

    twin = a == b
    gap = lax.rem(lax.rem(b, RING) - lax.rem(a, RING) + RING, RING)
    back = lax.rem(RING - gap, RING)
    def any_of(value, options):
        found = value < 0
        for option in options:
            found = jnp.logical_or(found, value == option)
        return found

    late = any_of(back, [d for d in range(RING) if NEAR[d] >= 2])
    step = jnp.int32(0)
    for d in range(RING):
        step = jnp.where(back == d, NEAR[d], step)
    out_0, out_1, out_2 = (
        any_of(gap, [(d - j) % RING for d in range(RING) if NEAR[d] == j]) for j in range(3)
    )
    not_twin = jnp.logical_not(twin)
    go_0 = jnp.logical_and(out_0, not_twin)

    barrier = pltpu.get_barrier_semaphore()

    def hello(device):
        pl.semaphore_signal(barrier, inc=1, device_id=device, device_id_type=MESH)

    i = lax.rem(a, HALF)
    z = lax.rem(b, HALF)
    over_row = at(a + HALF, b)
    over_col = at(a, b + HALF)

    for k in range(1, 4):
        hello(at(a, b + k))
        hello(at(b, a + k))

    @pl.when(z == HALF - 1)
    def _():
        hello(at(a, b - HALF + 1))

    @pl.when(z == 0)
    def _():
        hello(over_col)

    odd = lax.rem(a, 2) == 1
    hello(at(jnp.where(i + 1 >= HALF, a + 1 - HALF, a + 1), b))

    @pl.when(odd)
    def _():
        for k in range(2, 4):
            hello(at(jnp.where(i + k >= HALF, a + k - HALF, a + k), b))

    @pl.when(i <= 2)
    def _():
        hello(over_row)

    @pl.when(not_twin)
    def _():
        hello(at(b, a))
        hello(at(b, a - step))

    one = jnp.int32(1)
    zero = jnp.int32(0)
    expected = (
        jnp.where(z == 0, jnp.int32(8), jnp.int32(6))
        + jnp.where(i <= 2, jnp.int32(3), jnp.int32(2))
        + jnp.where(not_twin, one, zero)
        + jnp.where(go_0, one, zero)
        + jnp.where(out_1, one, zero)
        + jnp.where(out_2, one, zero)
    )
    pl.semaphore_wait(barrier, expected)

    size = SLOTS // CHUNKS

    def part(q):
        return pl.ds(q * size, size)

    def remote(src, dst, send, recv, device):
        return pltpu.make_async_remote_copy(
            src_ref=src, dst_ref=dst, send_sem=send, recv_sem=recv, device_id=device, device_id_type=MESH
        )

    def left_src(k, q):
        return x.at[part(q)] if k == 0 else L.at[k - 1, part(q)]

    def left(k, q):
        return remote(left_src(k, q), L.at[k, part(q)], l_send.at[k, q], l_recv.at[k, q], at(a, b - 1))

    def left_over(k, q):
        return remote(left_src(k, q), Y.at[k, part(q)], l_send.at[k, q], y_recv.at[k, q], over_col)

    def left_after(k, q):
        return remote(Y.at[k, part(q)], L.at[k, part(q)], y_send.at[k, q], l_recv.at[k, q], at(a, b + HALF - 1))

    def start_left(k, q):
        if q % 2 == 0:
            left(k, q).start()
        else:
            @pl.when(z == 0)
            def _():
                left_over(k, q).start()

            @pl.when(z != 0)
            def _():
                left(k, q).start()

    def cross_left(k, q):
        if q % 2 == 1:
            @pl.when(z == 0)
            def _():
                left_over(k, q).wait_recv()
                left_after(k, q).start()

    def mirror(j, q):
        src = x.at[part(q)] if j == 0 else L.at[j - 1, part(q)]
        return remote(src, R.at[0, part(q)], m_send.at[j, q], r_recv.at[0, q], at(b + j, a))

    def right(k, q):
        return remote(R.at[0, part(q)], R.at[k, part(q)], r_send.at[k, q], r_recv.at[k, q], at(a - k, b))

    def hand_on(k, q):
        return remote(R.at[k - 1, part(q)], R.at[k, part(q)], h_send.at[k - 2, q], r_recv.at[k, q], at(a - 1, b))

    def to_row(k, here):
        return here if k == 1 else jnp.logical_and(here, odd if k == 2 else jnp.logical_not(odd))

    def right_over(q):
        return remote(R.at[0, part(q)], X.at[part(q)], x_send.at[3, q], x_recv.at[q], over_row)

    def right_after(k, q):
        return remote(X.at[part(q)], R.at[k, part(q)], x_send.at[k - 1, q], r_recv.at[k, q], at(a + HALF - k, b))

    def live_left(k):
        return remote(live, lv.at[k], lv_send.at[k], lv_recv.at[k], at(a, b - 1 - k))

    def live_mirror(k):
        return remote(live, rv.at[k], rv_send.at[k], rv_recv.at[k], at(b - k, a))

    own = pltpu.make_async_copy(x, R.at[0], own_sem)

    for k in range(3):
        live_left(k).start()
        live_mirror(k + 1).start()

    @pl.when(not_twin)
    def _():
        live_mirror(0).start()

    @pl.when(twin)
    def _():
        own.start()

    for q in range(CHUNKS):
        @pl.when(go_0)
        def _():
            mirror(0, q).start()

        start_left(0, q)

    def take_mirror(q):
        @pl.when(not_twin)
        def _():
            mirror(0, q).wait_recv()

        @pl.when(i <= 2)
        def _():
            right_over(q).start()

        for k in range(1, 4):
            @pl.when(to_row(k, i >= k))
            def _():
                right(k, q).start()

    def cross_right(q):
        @pl.when(i <= 2)
        def _():
            right_over(q).wait_recv()

            for k in range(1, 4):
                @pl.when(to_row(k, i < k))
                def _():
                    right_after(k, q).start()

    def take_and_cross(q):
        take_mirror(q)
        if q > 0:
            cross_right(q - 1)
        if q == CHUNKS - 1:
            cross_right(q)

    for q in range(CHUNKS):
        if q > 0:
            cross_left(0, q - 1)
        left(0, q).wait_recv()

        @pl.when(out_1)
        def _():
            mirror(1, q).start()

        start_left(1, q)
    cross_left(0, CHUNKS - 1)

    for k in range(3):
        live_left(k).wait_recv()
        live_mirror(k + 1).wait_recv()

    @pl.when(not_twin)
    def _():
        live_mirror(0).wait_recv()

    lefts = [live[...], lv[0], lv[1], lv[2]]
    rights = [jnp.where(twin, live[...], rv[0]), rv[1], rv[2], rv[3]]
    make_list(pairs, counts, lefts, rights, listed, spans)

    @pl.when(twin)
    def _():
        own.wait()

    for q in range(CHUNKS):
        cross_left(1, q)

        @pl.when(jnp.logical_not(late))
        def _():
            take_and_cross(q)

        left(1, q).wait_recv()

        @pl.when(out_2)
        def _():
            mirror(2, q).start()

        start_left(2, q)

    for q in range(CHUNKS):
        cross_left(2, q)

        @pl.when(late)
        def _():
            take_and_cross(q)

    for q in range(CHUNKS):
        for k in range(1, 4):
            right(k, q).wait_recv()
            if k < 3:
                @pl.when(odd)
                def _():
                    hand_on(k + 1, q).start()

    for q in range(CHUNKS):
        left(2, q).wait_recv()

        @pl.when(odd)
        def _():
            hand_on(2, q).wait_send()
            hand_on(3, q).wait_send()

    for q in range(CHUNKS):
        for k in range(3):
            left(k, q).wait_send()
            if q % 2 == 1:
                @pl.when(z == 0)
                def _():
                    left_after(k, q).wait_send()

        for k in range(1, 4):
            @pl.when(to_row(k, i >= k))
            def _():
                right(k, q).wait_send()

            @pl.when(to_row(k, i < k))
            def _():
                right_after(k, q).wait_send()

        @pl.when(i <= 2)
        def _():
            right_over(q).wait_send()

        @pl.when(go_0)
        def _():
            mirror(0, q).wait_send()

        @pl.when(out_1)
        def _():
            mirror(1, q).wait_send()

        @pl.when(out_2)
        def _():
            mirror(2, q).wait_send()

    for k in range(3):
        live_left(k).wait_send()
        live_mirror(k + 1).wait_send()

    @pl.when(not_twin)
    def _():
        live_mirror(0).wait_send()


def moves(x, live, pairs, counts):
    dma = pltpu.SemaphoreType.DMA
    tile = (SLOTS, BLK, BLK)
    return pl.pallas_call(
        moves_kernel,
        out_shape=[
            jax.ShapeDtypeStruct((3,) + tile, jnp.bfloat16),
            jax.ShapeDtypeStruct((4,) + tile, jnp.bfloat16),
            jax.ShapeDtypeStruct(tile, jnp.bfloat16),
            jax.ShapeDtypeStruct((3,) + tile, jnp.bfloat16),
            jax.ShapeDtypeStruct((8, LISTED), jnp.int32),
            jax.ShapeDtypeStruct((8, GROUPS), jnp.int32),
        ],
        in_specs=[
            pl.BlockSpec(memory_space=pl.ANY),
            pl.BlockSpec(memory_space=pltpu.VMEM),
            pl.BlockSpec(memory_space=pltpu.VMEM),
            pl.BlockSpec(memory_space=pltpu.SMEM),
        ],
        out_specs=[
            pl.BlockSpec(memory_space=pl.ANY),
            pl.BlockSpec(memory_space=pl.ANY),
            pl.BlockSpec(memory_space=pl.ANY),
            pl.BlockSpec(memory_space=pl.ANY),
            pl.BlockSpec(memory_space=pltpu.VMEM),
            pl.BlockSpec(memory_space=pltpu.VMEM),
        ],
        scratch_shapes=[
            pltpu.VMEM((3, 1, SLOTS), jnp.int32),
            pltpu.VMEM((4, 1, SLOTS), jnp.int32),
            dma((3, CHUNKS)), dma((3, CHUNKS)),
            dma((4, CHUNKS)), dma((4, CHUNKS)),
            dma((3, CHUNKS)),
            dma((3,)), dma((3,)), dma((4,)), dma((4,)),
            dma((4, CHUNKS)), dma((CHUNKS,)), dma((3, CHUNKS)), dma((3, CHUNKS)),
            dma((2, CHUNKS)),
            dma,
        ],
        compiler_params=pltpu.CompilerParams(collective_id=0, has_side_effects=True),
        name="moves",
    )(x, live, pairs, counts)


def sums_kernel(listed, spans, x, L, R, out, left, right, total, in_sems, out_sem):
    copies = [
        pltpu.make_async_copy(x, left.at[pl.ds(1, SLOTS)], in_sems.at[0]),
        pltpu.make_async_copy(L, left.at[pl.ds(1 + SLOTS, 3 * SLOTS)], in_sems.at[1]),
        pltpu.make_async_copy(R, right.at[pl.ds(1, 4 * SLOTS)], in_sems.at[2]),
    ]
    for c in copies:
        c.start()
    left[0] = jnp.zeros((BLK, BLK), jnp.bfloat16)
    right[0] = jnp.zeros((BLK, BLK), jnp.bfloat16)

    for o in range(SLOTS):
        total[o] = jnp.zeros((BLK, BLK), jnp.float32)

    for c in copies:
        c.wait()

    def batch(i, carry):
        for u in range(BATCH):
            group = i * BATCH + u
            base = group * GROUP
            product = None
            for k in range(0, GROUP, GROUP):
                rows = jnp.concatenate([left[listed[0, base + n]] for n in range(GROUP)], axis=1)
                cols = jnp.concatenate([right[listed[1, base + n]] for n in range(GROUP)], axis=1)
                term = lax.dot_general(
                    rows, cols, (((1,), (1,)), ((), ())), preferred_element_type=jnp.float32
                )
                product = term if product is None else product + term
            total[spans[0, group]] += product
        return carry

    lax.fori_loop(0, lax.div(spans[1, 0] + (BATCH - 1), BATCH), batch, 0)
    done = pltpu.make_async_copy(total.at[pl.ds(0, SLOTS)], out, out_sem)
    done.start()
    done.wait()


def sums(listed, spans, x, L, R):
    return pl.pallas_call(
        sums_kernel,
        out_shape=jax.ShapeDtypeStruct((SLOTS, BLK, BLK), jnp.float32),
        in_specs=[pl.BlockSpec(memory_space=pltpu.SMEM)] * 2 + [pl.BlockSpec(memory_space=pl.ANY)] * 3,
        out_specs=pl.BlockSpec(memory_space=pl.ANY),
        scratch_shapes=[
            pltpu.VMEM((1 + 4 * SLOTS, BLK, BLK), jnp.bfloat16),
            pltpu.VMEM((1 + 4 * SLOTS, BLK, BLK), jnp.bfloat16),
            pltpu.VMEM((SLOTS + 1, BLK, BLK), jnp.float32),
            pltpu.SemaphoreType.DMA((3,)),
            pltpu.SemaphoreType.DMA,
        ],
        name="sums",
    )(listed, spans, x, L, R)


def body(x_blocks, x_live, pair_slots, pair_count):
    x = x_blocks[0, 0]
    L, R, _, _, listed, spans = moves(x, x_live[0], jnp.swapaxes(pair_slots[0, 0], 0, 1), pair_count[0, 0])
    gram = sums(listed, spans, x, L.reshape(3 * SLOTS, BLK, BLK), R.reshape(4 * SLOTS, BLK, BLK))
    return gram[None, None]


def solution(mesh):
    return jax.shard_map(
        body,
        mesh=mesh,
        in_specs=(
            P("row", "col", None, None, None),
            P("row", "col", None),
            P("row", "col", None, None, None),
            P("row", "col", None),
        ),
        out_specs=P("row", "col", None, None, None),
        check_vma=False,
    )
```
